32 devices in a mesh: groups: 2 (over y), depth: 4 (over z), rows: 2 (over x), cols: 2 (over core).
Axes of the slice: x: 2, y: 2, z: 4, core: 2. Of those that a mesh axis runs over, the one named last changes fastest.
Arguments:
- volume: bfloat16 [4, 16, 16, 3072], P('groups', 'depth', 'rows', 'cols'), parts along dimension 0, may hold values from -6 to 6
- grad_out: bfloat16 [4, 16, 16, 3072], P('groups', 'depth', 'rows', 'cols'), parts along dimension 0, may hold values from -6 to 6
- report: bfloat16 [1536], P('groups'), parts along dimension 0, may hold values from -6 to 6
- conv_kernel: bfloat16 [96, 1, 7, 7, 7], replicated, may hold values from -0.3125 to 0.3125
- conv_bias: float32 [96], replicated, may hold values from -4 to 4
- film_weight: bfloat16 [768, 192], replicated, may hold values from -0.21875 to 0.21875
- film_bias: float32 [192], replicated, may hold values from -3 to 3
- in_weight: bfloat16 [96, 384], replicated, may hold values from -0.625 to 0.625
- in_bias: float32 [384], replicated, may hold values from -3 to 3
- out_weight: bfloat16 [384, 96], replicated, may hold values from -0.3125 to 0.3125
Outputs:
- grad_input: bfloat16 [4, 16, 16, 3072], P('groups', 'depth', 'rows', 'cols'), parts along dimension 0
- grad_kernel: float32 [192, 1, 7, 7, 7], P('groups'), parts along dimension 0
- grad_conv_bias: float32 [192], P('groups'), parts along dimension 0
- grad_film: float32 [384], P('groups'), parts along dimension 0
- grad_in_weight: float32 [192, 384], P('groups'), parts along dimension 0
- grad_in_bias: float32 [768], P('groups'), parts along dimension 0
- grad_out_weight: float32 [768, 96], P('groups'), parts along dimension 0
The draws below stay inside these ranges and needn't reach their ends.
There are 2 independent parts, one for each index of `groups`. The reference program is written for one: setup_inputs(seed, part) draws one part's arguments, and reference() takes and returns one part's arrays. A program takes and returns all parts, laid end to end along the dimension named above; an argument that names none is the same for every part. Nothing has to cross between parts.
All inputs are finite; a program needn't handle non-finite values.
Results may differ from the reference program's by a relative error of at most 0.0062.
Values may be sent and summed in bfloat16 or wider, within the bound.
A program may use at most 64 MiB of HBM per device.

```python
import math
import jax
import jax.numpy as jnp
from jax import lax

C = 96
F = 384
E = 768
K = 7
B = 2
DEPTH = 16
HEIGHT = 16
WIDTH = 32
VOXELS = 8192
N_DEPTH = 4


def block_scale(stream_key, extent, shards, low, largest):
    def one(dim, parts):
        heights = jax.random.uniform(jax.random.fold_in(jax.random.fold_in(stream_key, 6), dim), (parts,), jnp.float32, low / len(shards), largest / len(shards))
        return jnp.repeat(jnp.exp(heights), extent[dim] // parts).reshape((-1,) + (1,) * (len(extent) - dim - 1))

    gain = one(*shards[0])
    for cut in shards[1:]:
        gain = gain * one(*cut)
    return gain


def noise(key, extent, spread, limit, shards=(), dtype=jnp.bfloat16):
    entries = spread * jax.random.normal(key, extent, jnp.float32)
    if shards:
        entries = entries * block_scale(key, extent, shards, -0.22, 0.18)
    return jnp.clip(entries, -limit, limit).astype(dtype)


def setup_inputs(seed: int = 0, part: int = 0) -> dict:
    key_of = jax.random.split(jax.random.key(seed), 11)
    part_splits = jax.random.split(jax.random.fold_in(key_of[10], part), 11)
    return {
        "volume": noise(part_splits[0], (B, DEPTH, HEIGHT, WIDTH * C), 1.0, 6.0, ((1, 4), (2, 2), (3, 2))),
        "grad_out": noise(part_splits[1], (B, DEPTH, HEIGHT, WIDTH * C), 1.0, 6.0, ((1, 4), (2, 2), (3, 2))),
        "report": noise(part_splits[2], (E,), 1.0, 6.0),
        "conv_kernel": noise(key_of[3], (C, 1, K, K, K), (K * K * K) ** -0.5, 0.3125),
        "conv_bias": noise(key_of[4], (C,), 1.0, 4.0, (), jnp.float32),
        "film_weight": noise(key_of[5], (E, 2 * C), E ** -0.5, 0.21875),
        "film_bias": noise(key_of[6], (2 * C,), 0.5, 3.0, (), jnp.float32),
        "in_weight": noise(key_of[7], (C, F), C ** -0.5, 0.625),
        "in_bias": noise(key_of[8], (F,), 0.5, 3.0, (), jnp.float32),
        "out_weight": noise(key_of[9], (F, C), F ** -0.5, 0.3125),
    }


epsilon = 1e-06
conv_dims = ('NCDHW', 'OIDHW', 'NCDHW')

def depthwise(padded, kernel):
    return lax.conv_general_dilated(padded[None], kernel, (1, 1, 1), 'VALID', dimension_numbers=conv_dims, feature_group_count=kernel.shape[0], preferred_element_type=jnp.float32)[0]

def pointwise(conv_flat, grad_flat, film_vec, in_weight, in_bias, out_weight):
    channels = conv_flat.shape[0]
    chan_mean = lax.optimization_barrier(jnp.mean(conv_flat, axis=0))
    centred = conv_flat - chan_mean
    variance = lax.optimization_barrier(jnp.mean(centred * centred, axis=0))
    inverse = lax.rsqrt(variance + epsilon)
    normed = centred * inverse
    scale_vec = 1.0 + film_vec[:channels, None]
    hidden_in = (normed * scale_vec + film_vec[channels:, None]).astype(jnp.bfloat16)
    pre_act = jnp.dot(in_weight.T, hidden_in, preferred_element_type=jnp.float32) + in_bias[:, None]
    post_act, gelu_back = jax.vjp(jax.nn.gelu, pre_act)
    act_low = post_act.astype(jnp.bfloat16)
    grad_act = jnp.dot(out_weight, grad_flat, preferred_element_type=jnp.float32)
    grad_pre = gelu_back(grad_act)[0]
    grad_low = grad_pre.astype(jnp.bfloat16)
    grad_hidden = jnp.dot(in_weight, grad_low, preferred_element_type=jnp.float32)
    grad_out_w = jnp.dot(act_low, grad_flat.T, preferred_element_type=jnp.float32)
    grad_in_w = jnp.dot(hidden_in, grad_low.T, preferred_element_type=jnp.float32)
    grad_in_b = lax.optimization_barrier(jnp.sum(grad_pre, axis=1))
    grad_film = jnp.concatenate([lax.optimization_barrier(jnp.sum(grad_hidden * normed, axis=1)), lax.optimization_barrier(jnp.sum(grad_hidden, axis=1))])
    grad_normed = grad_hidden * scale_vec
    slope = ((grad_normed - lax.optimization_barrier(jnp.mean(grad_normed, axis=0)) - normed * lax.optimization_barrier(jnp.mean(grad_normed * normed, axis=0))) * inverse).astype(jnp.bfloat16)
    return (slope, (grad_in_w, grad_in_b, grad_out_w, grad_film))

def channels_first(crop):
    return jnp.transpose(crop.reshape(DEPTH, HEIGHT, WIDTH, C), (3, 0, 1, 2))

def reference(volume, grad_out, report, conv_kernel, conv_bias, film_weight, film_bias, in_weight, in_bias, out_weight):
    half_width = K // 2
    film_vec = jnp.dot(report[None, :], film_weight, preferred_element_type=jnp.float32)[0] + film_bias
    pad_spec = ((0, 0), (half_width, half_width), (half_width, half_width), (half_width, half_width))
    flipped = conv_kernel[:, :, ::-1, ::-1, ::-1]

    def one_crop(crop_pair):
        crop = channels_first(crop_pair[0])
        crop_grad = channels_first(crop_pair[1])
        padded = jnp.pad(crop, pad_spec)
        conv_out = depthwise(padded, conv_kernel) + conv_bias[:, None, None, None]
        blocks = N_DEPTH
        conv_blocks = jnp.moveaxis(conv_out.reshape(C, blocks, -1), 1, 0)
        grad_blocks = jnp.moveaxis(crop_grad.reshape(C, blocks, -1), 1, 0)

        def one_block(block_pair):
            return pointwise(block_pair[0], block_pair[1], film_vec, in_weight, in_bias, out_weight)
        slope_blocks, block_grads = lax.map(one_block, (conv_blocks, grad_blocks))
        slope_vol = jnp.moveaxis(slope_blocks, 0, 1).reshape(crop.shape)
        totals = jax.tree.map(lambda stacked: lax.optimization_barrier(jnp.sum(stacked, axis=0)), block_grads)
        slope_pad = jnp.pad(slope_vol, pad_spec)
        crop_input = (crop_grad.astype(jnp.float32) + depthwise(slope_pad, flipped)).astype(jnp.bfloat16)
        crop_input = jnp.transpose(crop_input, (1, 2, 3, 0)).reshape(DEPTH, HEIGHT, WIDTH * C)
        kernel_sum = lax.conv_general_dilated(padded[None], slope_vol[:, None], (1, 1, 1), 'VALID', dimension_numbers=conv_dims, feature_group_count=C, preferred_element_type=jnp.float32).reshape(conv_kernel.shape)
        bias_sum = lax.optimization_barrier(jnp.sum(slope_vol.astype(jnp.float32), axis=(1, 2, 3)))
        return (crop_input, (kernel_sum, bias_sum) + tuple(totals))
    grad_input, crop_sums = lax.map(one_crop, (volume, grad_out))
    sums = jax.tree.map(lambda stacked: lax.optimization_barrier(jnp.sum(stacked, axis=0)), crop_sums)
    factor = 1.0 / math.sqrt(B * VOXELS)
    return (grad_input, sums[0] * factor, sums[1] * factor, sums[5] * factor, sums[2] * factor, sums[3] * factor, sums[4] * factor)
```

```python
import functools
import math

import jax
import jax.numpy as jnp
from jax import lax
from jax.experimental import pallas as pl
from jax.experimental.pallas import tpu as pltpu
from jax.sharding import PartitionSpec as P

K = 7
HALF = K // 2
LANES = 128
SUB = 8
TAPS = K * K * K
EPSILON = 1e-06
MESH = pl.DeviceIdType.MESH
GELU_C = math.sqrt(2.0 / math.pi)
DIRS = tuple((dz, dx) for dz in (-1, 0, 1) for dx in (-1, 0, 1) if (dz, dx) != (0, 0))


def both(*conds):
    out = conds[0]
    for cond in conds[1:]:
        out = jnp.logical_and(out, cond)
    return out


def source_cells(step, extent):
    return {-1: slice(0, HALF), 0: slice(0, extent), 1: slice(extent - HALF, extent)}[step]


def target_cells(step, extent):
    return {
        -1: slice(HALF + extent, 2 * HALF + extent),
        0: slice(HALF, HALF + extent),
        1: slice(0, HALF),
    }[step]


class Halo:
    def __init__(self, own, pad, sems, where, counts):
        self.own, self.pad = own, pad
        self.send, self.recv, self.col_send, self.col_recv = sems
        self.grp, self.z, self.x, self.c = where
        self.nz, self.nx, self.nc = counts
        self.extents = own.shape[1], own.shape[2], own.shape[3]

    def inside(self, dz, dx, dc):
        z, x, c = self.z + dz, self.x + dx, self.c + dc
        return both(z >= 0, z < self.nz, x >= 0, x < self.nx, c >= 0, c < self.nc)

    def plane(self, idx):
        dz, dx = DIRS[idx]
        depth, rows, tiles = self.extents
        return pltpu.make_async_remote_copy(
            src_ref=self.own.at[:, source_cells(dz, depth), source_cells(dx, rows)],
            dst_ref=self.pad.at[
                :, target_cells(dz, depth), target_cells(dx, rows), slice(1, tiles + 1)
            ],
            send_sem=self.send.at[idx],
            recv_sem=self.recv.at[idx],
            device_id=(self.grp, self.z + dz, self.x + dx, self.c),
            device_id_type=MESH,
        )

    def column(self, idx, side):
        dc = (-1, 1)[side]
        depth, rows, tiles = self.extents
        dst_tile = tiles + 1 if dc < 0 else 0
        if idx == len(DIRS):
            area = (slice(None), target_cells(0, depth), target_cells(0, rows))
            src = self.own.at[:, :, :, 0 if dc < 0 else tiles - 1]
        else:
            dz, dx = DIRS[idx]
            area = (slice(None), target_cells(dz, depth), target_cells(dx, rows))
            src = self.pad.at[area + (1 if dc < 0 else tiles,)]
        return pltpu.make_async_remote_copy(
            src_ref=src,
            dst_ref=self.pad.at[area + (dst_tile,)],
            send_sem=self.col_send.at[side, idx],
            recv_sem=self.col_recv.at[side, idx],
            device_id=(self.grp, self.z, self.x, self.c + dc),
            device_id_type=MESH,
        )

    def fill_edges(self):
        pad = self.pad
        depth, rows, tiles = self.extents

        def clear(cond, area):
            @pl.when(cond)
            def _():
                view = pad.at[area]
                view[...] = jnp.zeros(view.shape, view.dtype)

        every = slice(None)
        clear(self.z == 0, (every, slice(0, HALF)))
        clear(self.z == self.nz - 1, (every, slice(HALF + depth, 2 * HALF + depth)))
        clear(self.x == 0, (every, every, slice(0, HALF)))
        clear(self.x == self.nx - 1, (every, every, slice(HALF + rows, 2 * HALF + rows)))
        clear(self.c == 0, (every, every, every, slice(0, 1)))
        clear(self.c == self.nc - 1, (every, every, every, slice(tiles + 1, tiles + 2)))

    def start(self):
        for idx, (dz, dx) in enumerate(DIRS):
            @pl.when(self.inside(dz, dx, 0))
            def _():
                self.plane(idx).start()
        for side in range(2):
            @pl.when(self.inside(0, 0, (-1, 1)[side]))
            def _():
                self.column(len(DIRS), side).start()

    def centre(self):
        depth, rows, tiles = self.extents
        self.pad[:, HALF : HALF + depth, HALF : HALF + rows, 1 : tiles + 1] = self.own[...]

    def relay(self):
        for idx, (dz, dx) in enumerate(DIRS):
            @pl.when(self.inside(-dz, -dx, 0))
            def _():
                self.plane(idx).wait_recv()
                for side in range(2):
                    @pl.when(self.inside(-dz, -dx, (-1, 1)[side]))
                    def _():
                        self.column(idx, side).start()

    def finish(self):
        for idx, (dz, dx) in enumerate(DIRS + ((0, 0),)):
            for side in range(2):
                dc = (-1, 1)[side]

                @pl.when(self.inside(-dz, -dx, -dc))
                def _():
                    self.column(idx, side).wait_recv()

                @pl.when(self.inside(-dz, -dx, dc))
                def _():
                    self.column(idx, side).wait_send()

        for idx, (dz, dx) in enumerate(DIRS):
            @pl.when(self.inside(dz, dx, 0))
            def _():
                self.plane(idx).wait_send()


def widen(pad, wide):
    crops, depth = pad.shape[0], pad.shape[1]
    tiles = pad.shape[3]

    def one(step, _):
        crop, d = step // depth, step % depth
        for tile in range(tiles):
            wide[crop, d, :, tile * SUB : (tile + 1) * SUB, :] = pad[crop, d, :, tile].astype(
                jnp.float32
            )
        return 0

    lax.fori_loop(0, crops * depth, one, 0)


def conv_tile(wide, taps, crop, tile, extents, flip):
    depth, rows = extents[0], extents[1]

    def row_tap(j, accs):
        accs = list(accs)
        for k in range(K):
            jw, kw = (K - 1 - j, K - 1 - k) if flip else (j, k)
            weights = [taps[jw, kw, K - 1 - i if flip else i] for i in range(K)]
            start = (tile + 1) * SUB - HALF + k
            for h in range(rows):
                cells = [wide[crop, d, j + h, start : start + SUB, :] for d in range(depth + K - 1)]
                for d in range(depth):
                    acc = accs[d * rows + h]
                    for i in range(K):
                        acc = acc + cells[d + i] * weights[i]
                    accs[d * rows + h] = acc
        return tuple(accs)

    zero = jnp.zeros((SUB, LANES), jnp.float32)
    return lax.fori_loop(0, K, row_tap, (zero,) * (depth * rows))


def kernel(
    counts, channels, row_of,
    x_ref, g_ref, taps_ref, vec_ref, inw_ref, inb_ref, outw_ref,
    gi_ref, red_ref,
    xp, sp, so, wide, conv_s, slope_s, accw, accb, accf, part, part_low, inbox, mine, full,
    halo_sems_0, halo_sems_1, halo_sems_2, halo_sems_3,
    slope_sems_0, slope_sems_1, slope_sems_2, slope_sems_3,
    rs_send, rs_recv, ag_send, ag_recv,
):
    nz, nx, nc = counts
    total = nz * nx * nc
    grp, z, x, c = (lax.axis_index(name) for name in ("groups", "depth", "rows", "cols"))
    me = (z * nx + x) * nc + c
    crops, depth, rows, tiles = x_ref.shape[:4]
    extents = (depth, rows, tiles)
    voxels = depth * rows * SUB
    hidden = inw_ref.shape[1]
    chunk = part.shape[0] // total

    def peer(offset):
        other = lax.rem(me + offset, total)
        return other, (grp, other // (nx * nc), (other // nc) % nx, other % nc)

    barrier = pltpu.get_barrier_semaphore()

    def greet(offset, _):
        pl.semaphore_signal(barrier, inc=1, device_id=peer(offset)[1], device_id_type=MESH)
        return 0

    lax.fori_loop(1, total, greet, 0)
    where = (grp, z, x, c)
    halo_x = Halo(x_ref, xp, (halo_sems_0, halo_sems_1, halo_sems_2, halo_sems_3), where, counts)
    halo_s = Halo(so, sp, (slope_sems_0, slope_sems_1, slope_sems_2, slope_sems_3), where, counts)
    pl.semaphore_wait(barrier, total - 1)
    halo_x.start()
    halo_x.fill_edges()
    halo_x.centre()
    halo_s.fill_edges()
    accw[...] = jnp.zeros_like(accw)
    accb[...] = jnp.zeros_like(accb)
    accf[...] = jnp.zeros_like(accf)
    tail = row_of["end"] // SUB * SUB
    part[tail:, :] = jnp.zeros((part.shape[0] - tail, LANES), jnp.float32)
    halo_x.relay()
    halo_x.finish()
    widen(xp, wide)

    def forward(crop, _):
        for tile in range(tiles):
            accs = conv_tile(wide, taps_ref, crop, tile, extents, False)
            for d in range(depth):
                for h in range(rows):
                    conv_s[crop * tiles + tile, d, h] = accs[d * rows + h]
        return 0

    lax.fori_loop(0, crops, forward, 0)

    conv_bias, scale, shift = vec_ref[0:1, :], vec_ref[1:2, :], vec_ref[2:3, :]
    real = lax.broadcasted_iota(jnp.int32, (1, LANES), 1) < channels

    def mlp(step, _):
        crop, tile = step // tiles, step % tiles
        conv = conv_s[step].reshape(voxels, LANES) + conv_bias
        mean = jnp.sum(conv, axis=1, keepdims=True) * (1.0 / channels)
        centred = jnp.where(real, conv - mean, 0.0)
        variance = jnp.sum(centred * centred, axis=1, keepdims=True) * (1.0 / channels)
        inverse = lax.rsqrt(variance + EPSILON)
        normed = centred * inverse
        hidden_in = (normed * scale + shift).astype(jnp.bfloat16)
        grad = g_ref[crop, :, :, tile].astype(jnp.float32).reshape(voxels, LANES)
        grad = grad.astype(jnp.bfloat16)
        pre = jnp.dot(hidden_in, inw_ref[...], preferred_element_type=jnp.float32) + inb_ref[...]
        square = pre * pre
        th = jnp.tanh(GELU_C * (pre + 0.044715 * (square * pre)))
        act_low = (0.5 * pre * (1.0 + th)).astype(jnp.bfloat16)
        slope_act = 0.5 * (1.0 + th) + 0.5 * pre * (1.0 - th * th) * (
            GELU_C * (1.0 + (3.0 * 0.044715) * square)
        )
        grad_act = lax.dot_general(
            grad, outw_ref[...], (((1,), (1,)), ((), ())), preferred_element_type=jnp.float32
        )
        grad_pre = grad_act * slope_act
        grad_low = grad_pre.astype(jnp.bfloat16)
        grad_hidden = lax.dot_general(
            grad_low, inw_ref[...], (((1,), (1,)), ((), ())), preferred_element_type=jnp.float32
        )
        over_voxels = (((0,), (0,)), ((), ()))
        accw[0] += lax.dot_general(
            hidden_in, grad_low, over_voxels, preferred_element_type=jnp.float32
        )
        accw[1] += lax.dot_general(grad, act_low, over_voxels, preferred_element_type=jnp.float32)
        accb[0:1, :] += jnp.sum(grad_pre, axis=0, keepdims=True)
        accf[1:2, :] += jnp.sum(grad_hidden * normed, axis=0, keepdims=True)
        accf[2:3, :] += jnp.sum(grad_hidden, axis=0, keepdims=True)
        grad_normed = grad_hidden * scale
        mean_g = jnp.sum(grad_normed, axis=1, keepdims=True) * (1.0 / channels)
        mean_gn = jnp.sum(grad_normed * normed, axis=1, keepdims=True) * (1.0 / channels)
        slope = (grad_normed - mean_g - normed * mean_gn) * inverse
        slope = slope.astype(jnp.bfloat16).astype(jnp.float32)
        accf[0:1, :] += jnp.sum(slope, axis=0, keepdims=True)
        slope = slope.reshape(depth, rows, SUB, LANES)
        slope_s[step] = slope
        so[crop, :, :, tile] = slope.astype(jnp.bfloat16)
        return 0

    lax.fori_loop(0, crops * tiles, mlp, 0)
    halo_s.start()
    halo_s.centre()

    def kernel_grad(j, _):
        for k in range(K):
            def gather(crop, accs):
                accs = list(accs)
                for tile in range(tiles):
                    start = (tile + 1) * SUB - HALF + k
                    for h in range(rows):
                        cells = [
                            wide[crop, d, j + h, start : start + SUB, :]
                            for d in range(depth + K - 1)
                        ]
                        for d in range(depth):
                            slope = slope_s[crop * tiles + tile, d, h]
                            for i in range(K):
                                accs[i] = accs[i] + cells[d + i] * slope
                return tuple(accs)

            zero = jnp.zeros((SUB, LANES), jnp.float32)
            accs = lax.fori_loop(0, crops, gather, (zero,) * K)
            for i in range(K):
                row = row_of["kernel"] + (i * K + j) * K + k
                part[pl.ds(row, 1), :] = jnp.sum(accs[i], axis=0, keepdims=True)
        return 0

    lax.fori_loop(0, K, kernel_grad, 0)
    halo_s.relay()

    for which, name in enumerate(("in", "out")):
        for block in range(hidden // LANES):
            first = row_of[name] + block * channels
            part[first : first + channels, :] = accw[
                which, 0:channels, block * LANES : (block + 1) * LANES
            ]
    part[row_of["small"] : row_of["small"] + 3, :] = accf[0:3, :]
    for block in range(hidden // LANES):
        row = row_of["in_bias"] + block
        part[row : row + 1, :] = accb[0:1, block * LANES : (block + 1) * LANES]
    part_low[...] = part[...].astype(jnp.bfloat16)

    def scatter(offset):
        other, device = peer(offset)
        return pltpu.make_async_remote_copy(
            src_ref=part_low.at[pl.ds(pl.multiple_of(other * chunk, chunk), chunk)],
            dst_ref=inbox.at[offset],
            send_sem=rs_send.at[offset],
            recv_sem=rs_recv.at[offset],
            device_id=device,
            device_id_type=MESH,
        )

    my_rows = pl.ds(pl.multiple_of(me * chunk, chunk), chunk)

    def spread(offset):
        return pltpu.make_async_remote_copy(
            src_ref=mine,
            dst_ref=full.at[my_rows],
            send_sem=ag_send.at[offset],
            recv_sem=ag_recv.at[offset],
            device_id=peer(offset)[1],
            device_id_type=MESH,
        )

    def arrived(offset):
        origin = lax.rem(me + total - offset, total)
        return pltpu.make_async_remote_copy(
            src_ref=mine,
            dst_ref=full.at[pl.ds(pl.multiple_of(origin * chunk, chunk), chunk)],
            send_sem=ag_send.at[offset],
            recv_sem=ag_recv.at[offset],
            device_id=peer(offset)[1],
            device_id_type=MESH,
        )

    def each(fn):
        def step(offset, _):
            fn(offset)
            return 0

        lax.fori_loop(1, total, step, 0)

    each(lambda offset: scatter(offset).start())
    halo_s.finish()
    widen(sp, wide)

    def backward(crop):
        for tile in range(tiles):
            accs = conv_tile(wide, taps_ref, crop, tile, extents, True)
            for d in range(depth):
                for h in range(rows):
                    grad = g_ref[crop, d, h, tile].astype(jnp.float32)
                    gi_ref[crop, d, h, tile] = (grad + accs[d * rows + h]).astype(jnp.bfloat16)

    def backward_loop(first, last):
        def step(crop, _):
            backward(crop)
            return 0

        lax.fori_loop(first, last, step, 0)

    backward_loop(0, crops // 2)

    each(lambda offset: scatter(offset).wait())

    def add(offset, acc):
        return acc + inbox[offset].astype(jnp.float32)

    summed = lax.fori_loop(1, total, add, part[my_rows, :])
    mine[...] = summed.astype(jnp.bfloat16)
    full[my_rows, :] = mine[...]
    each(lambda offset: spread(offset).start())
    backward_loop(crops // 2, crops)

    def settle(offset):
        spread(offset).wait_send()
        arrived(offset).wait_recv()

    each(settle)
    red_ref[...] = full[...].astype(jnp.float32)


def local(
    counts, volume, grad_out, report, conv_kernel, conv_bias,
    film_weight, film_bias, in_weight, in_bias, out_weight,
):
    crops, slices, lines, merged = volume.shape
    channels = conv_kernel.shape[0]
    hidden = in_weight.shape[1]
    width = merged // channels
    tiles = width // SUB
    extra = LANES - channels
    block = (crops, slices, lines, tiles, SUB, LANES)

    def to_block(array):
        array = array.reshape(crops, slices, lines, tiles, SUB, channels)
        return jnp.pad(array, ((0, 0),) * 5 + ((0, extra),))

    film = jnp.dot(report[None, :], film_weight, preferred_element_type=jnp.float32)[0] + film_bias
    vecs = jnp.stack([conv_bias, 1.0 + film[:channels], film[channels:]])
    vecs = jnp.pad(vecs, ((0, SUB - 3), (0, extra)))
    taps = jnp.transpose(conv_kernel[:, 0].astype(jnp.float32), (2, 3, 1, 0))
    taps = jnp.broadcast_to(
        jnp.pad(taps, ((0, 0),) * 3 + ((0, extra),))[:, :, :, None, :], (K, K, K, SUB, LANES)
    )
    total = counts[0] * counts[1] * counts[2]
    blocks = hidden // LANES
    row_of = {"in": 0, "out": blocks * channels, "kernel": 2 * blocks * channels}
    row_of["small"] = row_of["kernel"] + TAPS
    row_of["in_bias"] = row_of["small"] + 3
    row_of["end"] = row_of["in_bias"] + blocks
    unit = 16 * total
    all_rows = -(-row_of["end"] // unit) * unit
    chunk = all_rows // total
    padded = (crops, slices + 2 * HALF, lines + 2 * HALF, tiles + 2, SUB, LANES)
    bf, f32 = jnp.bfloat16, jnp.float32
    dma = pltpu.SemaphoreType.DMA
    halo_sems = [dma((len(DIRS),))] * 2 + [dma((2, len(DIRS) + 1))] * 2
    grad_input, red = pl.pallas_call(
        functools.partial(kernel, counts, channels, row_of),
        out_shape=(
            jax.ShapeDtypeStruct(block, bf),
            jax.ShapeDtypeStruct((all_rows, LANES), f32),
        ),
        in_specs=[pl.BlockSpec(memory_space=pltpu.VMEM)] * 7,
        out_specs=(pl.BlockSpec(memory_space=pltpu.VMEM),) * 2,
        scratch_shapes=[
            pltpu.VMEM(padded, bf),
            pltpu.VMEM(padded, bf),
            pltpu.VMEM(block, bf),
            pltpu.VMEM(padded[:3] + (padded[3] * SUB, LANES), f32),
            pltpu.VMEM((crops * tiles, slices, lines, SUB, LANES), f32),
            pltpu.VMEM((crops * tiles, slices, lines, SUB, LANES), f32),
            pltpu.VMEM((2, LANES, hidden), f32),
            pltpu.VMEM((SUB, hidden), f32),
            pltpu.VMEM((SUB, LANES), f32),
            pltpu.VMEM((all_rows, LANES), f32),
            pltpu.VMEM((all_rows, LANES), bf),
            pltpu.VMEM((total, chunk, LANES), bf),
            pltpu.VMEM((chunk, LANES), bf),
            pltpu.VMEM((all_rows, LANES), bf),
        ]
        + halo_sems
        + halo_sems
        + [dma((total,))] * 4,
        compiler_params=pltpu.CompilerParams(
            collective_id=0, has_side_effects=True, vmem_limit_bytes=56 * 1024 * 1024
        ),
        name="block",
    )(
        to_block(volume),
        to_block(grad_out),
        taps,
        vecs,
        jnp.pad(in_weight, ((0, extra), (0, 0))),
        in_bias[None, :],
        jnp.pad(out_weight, ((0, 0), (0, extra))),
    )
    grad_input = grad_input[..., :channels].reshape(volume.shape)
    factor = 1.0 / math.sqrt(crops * slices * lines * width * total)
    red = red * factor

    def matrix(name):
        rows = red[row_of[name] : row_of[name] + blocks * channels, :]
        return rows.reshape(blocks, channels, LANES)

    grad_in_w = jnp.transpose(matrix("in"), (1, 0, 2)).reshape(channels, hidden)
    grad_out_w = jnp.transpose(matrix("out")[:, :, :], (0, 2, 1)).reshape(hidden, channels)
    grad_kernel = red[row_of["kernel"] : row_of["kernel"] + TAPS, :channels].T
    grad_kernel = grad_kernel.reshape(channels, 1, K, K, K)
    small = red[row_of["small"] : row_of["small"] + 3, :channels]
    grad_film = jnp.concatenate([small[1], small[2]])
    grad_in_b = red[row_of["in_bias"] : row_of["in_bias"] + blocks, :].reshape(hidden)
    return grad_input, grad_kernel, small[0], grad_film, grad_in_w, grad_in_b, grad_out_w


def solution(mesh):
    split = P("groups", "depth", "rows", "cols")
    in_specs = (split, split, P("groups")) + (P(),) * 7
    out_specs = (
        split,
        P("groups", None, None, None, None),
        P("groups"),
        P("groups"),
        P("groups", None),
        P("groups"),
        P("groups", None),
    )
    counts = tuple(mesh.shape[name] for name in ("depth", "rows", "cols"))
    return jax.shard_map(
        functools.partial(local, counts),
        mesh=mesh,
        in_specs=in_specs,
        out_specs=out_specs,
        check_vma=False,
    )
```

```python
import functools
import math

import jax
import jax.numpy as jnp
from jax import lax
from jax.experimental import pallas as pl
from jax.experimental.pallas import tpu as pltpu
from jax.sharding import PartitionSpec as P

K = 7
HALF = K // 2
LANES = 128
SUB = 8
TAPS = K * K * K
EPSILON = 1e-06
MESH = pl.DeviceIdType.MESH
GELU_C = math.sqrt(2.0 / math.pi)
DIRS = tuple((dz, dx) for dz in (-1, 0, 1) for dx in (-1, 0, 1) if (dz, dx) != (0, 0))


def both(*conds):
    out = conds[0]
    for cond in conds[1:]:
        out = jnp.logical_and(out, cond)
    return out


def source_cells(step, extent):
    return {-1: slice(0, HALF), 0: slice(0, extent), 1: slice(extent - HALF, extent)}[step]


def target_cells(step, extent):
    return {
        -1: slice(HALF + extent, 2 * HALF + extent),
        0: slice(HALF, HALF + extent),
        1: slice(0, HALF),
    }[step]


class Halo:
    def __init__(self, own, pad, sems, where, counts):
        self.own, self.pad = own, pad
        self.send, self.recv, self.col_send, self.col_recv = sems
        self.grp, self.z, self.x, self.c = where
        self.nz, self.nx, self.nc = counts
        self.extents = own.shape[1], own.shape[2], own.shape[3]

    def inside(self, dz, dx, dc):
        z, x, c = self.z + dz, self.x + dx, self.c + dc
        return both(z >= 0, z < self.nz, x >= 0, x < self.nx, c >= 0, c < self.nc)

    def plane(self, idx):
        dz, dx = DIRS[idx]
        depth, rows, tiles = self.extents
        return pltpu.make_async_remote_copy(
            src_ref=self.own.at[:, source_cells(dz, depth), source_cells(dx, rows)],
            dst_ref=self.pad.at[
                :, target_cells(dz, depth), target_cells(dx, rows), slice(1, tiles + 1)
            ],
            send_sem=self.send.at[idx],
            recv_sem=self.recv.at[idx],
            device_id=(self.grp, self.z + dz, self.x + dx, self.c),
            device_id_type=MESH,
        )

    def column(self, idx, side):
        dc = (-1, 1)[side]
        depth, rows, tiles = self.extents
        dst_tile = tiles + 1 if dc < 0 else 0
        if idx == len(DIRS):
            area = (slice(None), target_cells(0, depth), target_cells(0, rows))
            src = self.own.at[:, :, :, 0 if dc < 0 else tiles - 1]
        else:
            dz, dx = DIRS[idx]
            area = (slice(None), target_cells(dz, depth), target_cells(dx, rows))
            src = self.pad.at[area + (1 if dc < 0 else tiles,)]
        return pltpu.make_async_remote_copy(
            src_ref=src,
            dst_ref=self.pad.at[area + (dst_tile,)],
            send_sem=self.col_send.at[side, idx],
            recv_sem=self.col_recv.at[side, idx],
            device_id=(self.grp, self.z, self.x, self.c + dc),
            device_id_type=MESH,
        )

    def fill_edges(self):
        pad = self.pad
        depth, rows, tiles = self.extents

        def clear(cond, area):
            @pl.when(cond)
            def _():
                view = pad.at[area]
                view[...] = jnp.zeros(view.shape, view.dtype)

        every = slice(None)
        clear(self.z == 0, (every, slice(0, HALF)))
        clear(self.z == self.nz - 1, (every, slice(HALF + depth, 2 * HALF + depth)))
        clear(self.x == 0, (every, every, slice(0, HALF)))
        clear(self.x == self.nx - 1, (every, every, slice(HALF + rows, 2 * HALF + rows)))
        clear(self.c == 0, (every, every, every, slice(0, 1)))
        clear(self.c == self.nc - 1, (every, every, every, slice(tiles + 1, tiles + 2)))

    def start(self):
        for idx, (dz, dx) in enumerate(DIRS):
            @pl.when(self.inside(dz, dx, 0))
            def _():
                self.plane(idx).start()
        for side in range(2):
            @pl.when(self.inside(0, 0, (-1, 1)[side]))
            def _():
                self.column(len(DIRS), side).start()

    def centre(self):
        depth, rows, tiles = self.extents
        self.pad[:, HALF : HALF + depth, HALF : HALF + rows, 1 : tiles + 1] = self.own[...]

    def relay(self):
        for idx, (dz, dx) in enumerate(DIRS):
            @pl.when(self.inside(-dz, -dx, 0))
            def _():
                self.plane(idx).wait_recv()
                for side in range(2):
                    @pl.when(self.inside(-dz, -dx, (-1, 1)[side]))
                    def _():
                        self.column(idx, side).start()

    def finish(self):
        for idx, (dz, dx) in enumerate(DIRS + ((0, 0),)):
            for side in range(2):
                dc = (-1, 1)[side]

                @pl.when(self.inside(-dz, -dx, -dc))
                def _():
                    self.column(idx, side).wait_recv()

                @pl.when(self.inside(-dz, -dx, dc))
                def _():
                    self.column(idx, side).wait_send()

        for idx, (dz, dx) in enumerate(DIRS):
            @pl.when(self.inside(dz, dx, 0))
            def _():
                self.plane(idx).wait_send()


def widen(pad, wide):
    crops, depth = pad.shape[0], pad.shape[1]
    tiles = pad.shape[3]

    def one(step, _):
        crop, d = step // depth, step % depth
        for tile in range(tiles):
            wide[crop, d, :, tile * SUB : (tile + 1) * SUB, :] = pad[crop, d, :, tile].astype(
                jnp.float32
            )
        return 0

    lax.fori_loop(0, crops * depth, one, 0)


def conv_tile(wide, taps, crop, tile, extents, flip):
    depth, rows = extents[0], extents[1]

    def row_tap(j, accs):
        accs = list(accs)
        for k in range(K):
            jw, kw = (K - 1 - j, K - 1 - k) if flip else (j, k)
            weights = [taps[jw, kw, K - 1 - i if flip else i] for i in range(K)]
            start = (tile + 1) * SUB - HALF + k
            for h in range(rows):
                cells = [wide[crop, d, j + h, start : start + SUB, :] for d in range(depth + K - 1)]
                for d in range(depth):
                    acc = accs[d * rows + h]
                    for i in range(K):
                        acc = acc + cells[d + i] * weights[i]
                    accs[d * rows + h] = acc
        return tuple(accs)

    zero = jnp.zeros((SUB, LANES), jnp.float32)
    return lax.fori_loop(0, K, row_tap, (zero,) * (depth * rows))


def kernel(
    counts, channels, row_of,
    factor, x_raw, g_raw, kernel_ref, bias_ref, report_ref, fw_ref, small_ref, inw_raw, outw_raw,
    gi_ref, gk_ref, gb_ref, gsmall_ref, ginw_ref, goutw_ref,
    x_ref, g_ref, taps_ref, inw_ref, outw_ref, red_ref, xp, sp, so, wide, conv_s, slope_s, vec_ref, accw, accb, accf, part, part_low, inbox, mine, full,
    halo_sems_0, halo_sems_1, halo_sems_2, halo_sems_3,
    slope_sems_0, slope_sems_1, slope_sems_2, slope_sems_3,
    rs_send, rs_recv, ag_send, ag_recv,
):
    nz, nx, nc = counts
    total = nz * nx * nc
    grp, z, x, c = (lax.axis_index(name) for name in ("groups", "depth", "rows", "cols"))
    me = (z * nx + x) * nc + c
    crops, depth, rows, tiles = x_raw.shape[:4]
    extents = (depth, rows, tiles)
    voxels = depth * rows * SUB
    hidden = inw_raw.shape[1]
    chunk = part.shape[0] // total

    def peer(offset):
        other = lax.rem(me + offset, total)
        return other, (grp, other // (nx * nc), (other // nc) % nx, other % nc)

    barrier = pltpu.get_barrier_semaphore()

    def greet(offset, _):
        pl.semaphore_signal(barrier, inc=1, device_id=peer(offset)[1], device_id_type=MESH)
        return 0

    lax.fori_loop(1, total, greet, 0)
    spare = LANES - channels
    x_ref[..., 0:channels] = x_raw[...]
    x_ref[..., channels:] = jnp.zeros(x_ref.shape[:-1] + (spare,), jnp.bfloat16)
    where = (grp, z, x, c)
    halo_x = Halo(x_ref, xp, (halo_sems_0, halo_sems_1, halo_sems_2, halo_sems_3), where, counts)
    halo_s = Halo(so, sp, (slope_sems_0, slope_sems_1, slope_sems_2, slope_sems_3), where, counts)
    pl.semaphore_wait(barrier, total - 1)
    halo_x.start()
    halo_x.fill_edges()
    halo_x.centre()
    halo_s.fill_edges()
    g_ref[..., 0:channels] = g_raw[...]
    g_ref[..., channels:] = jnp.zeros(g_ref.shape[:-1] + (spare,), jnp.bfloat16)
    for raw, ready in ((inw_raw, inw_ref), (outw_raw, outw_ref)):
        ready[0:channels, :] = raw[...]
        ready[channels:, :] = jnp.zeros((spare, hidden), jnp.bfloat16)
    taps_ref[...] = jnp.zeros_like(taps_ref)

    def tap_rows(ij, _):
        i, j = ij // K, ij % K
        rows_k = kernel_ref[i, j].astype(jnp.float32)
        for k in range(K):
            taps_ref[j, k, i, :, 0:channels] = jnp.broadcast_to(
                rows_k[k : k + 1, :], (SUB, channels)
            )
        return 0

    lax.fori_loop(0, K * K, tap_rows, 0)
    vec_ref[...] = jnp.zeros_like(vec_ref)
    vec_ref[0:1, 0:channels] = bias_ref[...]
    for half in range(2):
        film = lax.dot_general(
            report_ref[...], fw_ref[half * channels : (half + 1) * channels, :],
            (((1,), (1,)), ((), ())), preferred_element_type=jnp.float32,
        )
        film = film + small_ref[half : half + 1, 0:channels]
        vec_ref[half + 1 : half + 2, 0:channels] = film + (1.0 if half == 0 else 0.0)
    accw[...] = jnp.zeros_like(accw)
    accb[...] = jnp.zeros_like(accb)
    accf[...] = jnp.zeros_like(accf)
    tail = row_of["kernel"]
    part[tail:, :] = jnp.zeros((part.shape[0] - tail, LANES), jnp.float32)
    halo_x.relay()
    halo_x.finish()
    widen(xp, wide)

    def forward(crop, _):
        for tile in range(tiles):
            accs = conv_tile(wide, taps_ref, crop, tile, extents, False)
            for d in range(depth):
                for h in range(rows):
                    conv_s[crop * tiles + tile, d, h] = accs[d * rows + h]
        return 0

    lax.fori_loop(0, crops, forward, 0)

    conv_bias, scale, shift = vec_ref[0:1, :], vec_ref[1:2, :], vec_ref[2:3, :]
    in_bias = jnp.concatenate(
        [small_ref[2 + b : 3 + b, :] for b in range(hidden // LANES)], axis=1
    )
    real = lax.broadcasted_iota(jnp.int32, (1, LANES), 1) < channels

    def mlp(step, _):
        crop, tile = step // tiles, step % tiles
        conv = conv_s[step].reshape(voxels, LANES) + conv_bias
        mean = jnp.sum(conv, axis=1, keepdims=True) * (1.0 / channels)
        centred = jnp.where(real, conv - mean, 0.0)
        variance = jnp.sum(centred * centred, axis=1, keepdims=True) * (1.0 / channels)
        inverse = lax.rsqrt(variance + EPSILON)
        normed = centred * inverse
        hidden_in = (normed * scale + shift).astype(jnp.bfloat16)
        grad = g_ref[crop, :, :, tile].astype(jnp.float32).reshape(voxels, LANES)
        grad = grad.astype(jnp.bfloat16)
        pre = jnp.dot(hidden_in, inw_ref[...], preferred_element_type=jnp.float32) + in_bias
        square = pre * pre
        th = jnp.tanh(GELU_C * (pre + 0.044715 * (square * pre)))
        act_low = (0.5 * pre * (1.0 + th)).astype(jnp.bfloat16)
        slope_act = 0.5 * (1.0 + th) + 0.5 * pre * (1.0 - th * th) * (
            GELU_C * (1.0 + (3.0 * 0.044715) * square)
        )
        grad_act = jnp.dot(grad, outw_ref[...], preferred_element_type=jnp.float32)
        grad_pre = grad_act * slope_act
        grad_low = grad_pre.astype(jnp.bfloat16)
        grad_hidden = lax.dot_general(
            grad_low, inw_ref[...], (((1,), (1,)), ((), ())), preferred_element_type=jnp.float32
        )
        over_voxels = (((0,), (0,)), ((), ()))
        accw[0] += lax.dot_general(
            hidden_in, grad_low, over_voxels, preferred_element_type=jnp.float32
        )
        accw[1] += lax.dot_general(grad, act_low, over_voxels, preferred_element_type=jnp.float32)
        accb[0:1, :] += jnp.sum(grad_pre, axis=0, keepdims=True)
        accf[1:2, :] += jnp.sum(grad_hidden * normed, axis=0, keepdims=True)
        accf[2:3, :] += jnp.sum(grad_hidden, axis=0, keepdims=True)
        grad_normed = grad_hidden * scale
        mean_g = jnp.sum(grad_normed, axis=1, keepdims=True) * (1.0 / channels)
        mean_gn = jnp.sum(grad_normed * normed, axis=1, keepdims=True) * (1.0 / channels)
        slope = (grad_normed - mean_g - normed * mean_gn) * inverse
        slope = slope.astype(jnp.bfloat16).astype(jnp.float32)
        accf[0:1, :] += jnp.sum(slope, axis=0, keepdims=True)
        slope = slope.reshape(depth, rows, SUB, LANES)
        slope_s[step] = slope
        so[crop, :, :, tile] = slope.astype(jnp.bfloat16)
        return 0

    lax.fori_loop(0, crops * tiles, mlp, 0)
    halo_s.start()
    halo_s.centre()

    def kernel_grad(j, _):
        for k in range(K):
            def gather(crop, accs):
                accs = list(accs)
                for tile in range(tiles):
                    start = (tile + 1) * SUB - HALF + k
                    for h in range(rows):
                        cells = [
                            wide[crop, d, j + h, start : start + SUB, :]
                            for d in range(depth + K - 1)
                        ]
                        for d in range(depth):
                            slope = slope_s[crop * tiles + tile, d, h]
                            for i in range(K):
                                accs[i] = accs[i] + cells[d + i] * slope
                return tuple(accs)

            zero = jnp.zeros((SUB, LANES), jnp.float32)
            accs = lax.fori_loop(0, crops, gather, (zero,) * K)
            for i in range(K):
                row = row_of["kernel"] + (i * K + j) * SUB + k
                part[pl.ds(row, 1), :] = jnp.sum(accs[i], axis=0, keepdims=True)
        return 0

    lax.fori_loop(0, K, kernel_grad, 0)
    halo_s.relay()

    for which, name in enumerate(("in", "out")):
        for block in range(hidden // LANES):
            first = row_of[name] + block * channels
            part[first : first + channels, :] = accw[
                which, 0:channels, block * LANES : (block + 1) * LANES
            ]
    part[row_of["small"] : row_of["small"] + 3, :] = accf[0:3, :]
    for block in range(hidden // LANES):
        row = row_of["in_bias"] + block
        part[row : row + 1, :] = accb[0:1, block * LANES : (block + 1) * LANES]
    part_low[...] = part[...].astype(jnp.bfloat16)

    def scatter(offset):
        other, device = peer(offset)
        return pltpu.make_async_remote_copy(
            src_ref=part_low.at[pl.ds(pl.multiple_of(other * chunk, chunk), chunk)],
            dst_ref=inbox.at[offset],
            send_sem=rs_send.at[offset],
            recv_sem=rs_recv.at[offset],
            device_id=device,
            device_id_type=MESH,
        )

    my_rows = pl.ds(pl.multiple_of(me * chunk, chunk), chunk)

    def spread(offset):
        return pltpu.make_async_remote_copy(
            src_ref=mine,
            dst_ref=full.at[my_rows],
            send_sem=ag_send.at[offset],
            recv_sem=ag_recv.at[offset],
            device_id=peer(offset)[1],
            device_id_type=MESH,
        )

    def arrived(offset):
        origin = lax.rem(me + total - offset, total)
        return pltpu.make_async_remote_copy(
            src_ref=mine,
            dst_ref=full.at[pl.ds(pl.multiple_of(origin * chunk, chunk), chunk)],
            send_sem=ag_send.at[offset],
            recv_sem=ag_recv.at[offset],
            device_id=peer(offset)[1],
            device_id_type=MESH,
        )

    def each(fn):
        def step(offset, _):
            fn(offset)
            return 0

        lax.fori_loop(1, total, step, 0)

    each(lambda offset: scatter(offset).start())
    halo_s.finish()
    widen(sp, wide)

    def backward(crop):
        for tile in range(tiles):
            accs = conv_tile(wide, taps_ref, crop, tile, extents, True)
            for d in range(depth):
                for h in range(rows):
                    grad = g_ref[crop, d, h, tile].astype(jnp.float32)
                    total_in = grad + accs[d * rows + h]
                    gi_ref[crop, d, h, tile] = total_in[:, 0:channels].astype(jnp.bfloat16)

    def backward_loop(first, last):
        def step(crop, _):
            backward(crop)
            return 0

        lax.fori_loop(first, last, step, 0)

    backward_loop(0, crops // 2)

    each(lambda offset: scatter(offset).wait())

    def add(offset, acc):
        return acc + inbox[offset].astype(jnp.float32)

    summed = lax.fori_loop(1, total, add, part[my_rows, :])
    mine[...] = summed.astype(jnp.bfloat16)
    full[my_rows, :] = mine[...]
    each(lambda offset: spread(offset).start())
    backward_loop(crops // 2, crops)

    def settle(offset):
        spread(offset).wait_send()
        arrived(offset).wait_recv()

    each(settle)
    red_ref[...] = full[...].astype(jnp.float32) * factor
    for name, out_ref in (("in", ginw_ref), ("out", goutw_ref)):
        for block in range(hidden // LANES):
            first = row_of[name] + block * channels
            out_ref[:, block * LANES : (block + 1) * LANES] = red_ref[first : first + channels, :]
    for ij in range(K * K):
        first = row_of["kernel"] + ij * SUB
        gk_ref[ij // K, ij % K] = red_ref[first : first + K, 0:channels]
    gb_ref[...] = red_ref[row_of["small"] : row_of["small"] + 1, 0:channels]
    gsmall_ref[...] = red_ref[row_of["small"] : row_of["small"] + SUB, :]


def local(
    counts, volume, grad_out, report, conv_kernel, conv_bias,
    film_weight, film_bias, in_weight, in_bias, out_weight,
):
    crops, slices, lines, merged = volume.shape
    channels = conv_kernel.shape[0]
    hidden = in_weight.shape[1]
    width = merged // channels
    tiles = width // SUB
    extra = LANES - channels
    block = (crops, slices, lines, tiles, SUB, channels)
    wide_block = block[:-1] + (LANES,)

    def to_block(array):
        return array.reshape(block)

    smalls = jnp.concatenate(
        [
            jnp.pad(film_bias.reshape(2, channels), ((0, 0), (0, extra))),
            in_bias.reshape(hidden // LANES, LANES),
        ]
    )
    raw_kernel = jnp.transpose(conv_kernel[:, 0], (1, 2, 3, 0))
    total = counts[0] * counts[1] * counts[2]
    blocks = hidden // LANES
    row_of = {"in": 0, "out": blocks * channels, "kernel": 2 * blocks * channels}
    row_of["small"] = row_of["kernel"] + K * K * SUB
    row_of["in_bias"] = row_of["small"] + 3
    row_of["end"] = row_of["in_bias"] + -(-(blocks + 3) // SUB) * SUB
    unit = 16 * total
    all_rows = -(-row_of["end"] // unit) * unit
    chunk = all_rows // total
    padded = (crops, slices + 2 * HALF, lines + 2 * HALF, tiles + 2, SUB, LANES)
    bf, f32 = jnp.bfloat16, jnp.float32
    dma = pltpu.SemaphoreType.DMA
    halo_sems = [dma((len(DIRS),))] * 2 + [dma((2, len(DIRS) + 1))] * 2
    factor = 1.0 / math.sqrt(crops * slices * lines * width * total)
    grad_input, grad_kernel, grad_bias, smalls_out, grad_in_w, grad_out_w = pl.pallas_call(
        functools.partial(kernel, counts, channels, row_of, factor),
        out_shape=(
            jax.ShapeDtypeStruct(block, bf),
            jax.ShapeDtypeStruct((K, K, K, channels), f32),
            jax.ShapeDtypeStruct((1, channels), f32),
            jax.ShapeDtypeStruct((SUB, LANES), f32),
            jax.ShapeDtypeStruct((channels, hidden), f32),
            jax.ShapeDtypeStruct((channels, hidden), f32),
        ),
        in_specs=[pl.BlockSpec(memory_space=pltpu.VMEM)] * 9,
        out_specs=(pl.BlockSpec(memory_space=pltpu.VMEM),) * 6,
        scratch_shapes=[
            pltpu.VMEM(wide_block, bf),
            pltpu.VMEM(wide_block, bf),
            pltpu.VMEM((K, K, K, SUB, LANES), f32),
            pltpu.VMEM((LANES, hidden), bf),
            pltpu.VMEM((LANES, hidden), bf),
            pltpu.VMEM((all_rows, LANES), f32),
            pltpu.VMEM(padded, bf),
            pltpu.VMEM(padded, bf),
            pltpu.VMEM(wide_block, bf),
            pltpu.VMEM(padded[:3] + (padded[3] * SUB, LANES), f32),
            pltpu.VMEM((crops * tiles, slices, lines, SUB, LANES), f32),
            pltpu.VMEM((crops * tiles, slices, lines, SUB, LANES), f32),
            pltpu.VMEM((SUB, LANES), f32),
            pltpu.VMEM((2, LANES, hidden), f32),
            pltpu.VMEM((SUB, hidden), f32),
            pltpu.VMEM((SUB, LANES), f32),
            pltpu.VMEM((all_rows, LANES), f32),
            pltpu.VMEM((all_rows, LANES), bf),
            pltpu.VMEM((total, chunk, LANES), bf),
            pltpu.VMEM((chunk, LANES), bf),
            pltpu.VMEM((all_rows, LANES), bf),
        ]
        + halo_sems
        + halo_sems
        + [dma((total,))] * 4,
        compiler_params=pltpu.CompilerParams(
            collective_id=0, has_side_effects=True, vmem_limit_bytes=56 * 1024 * 1024
        ),
        name="block",
    )(
        to_block(volume),
        to_block(grad_out),
        raw_kernel,
        conv_bias[None, :],
        report[None, :],
        film_weight.T,
        smalls,
        in_weight,
        out_weight.T,
    )
    grad_input = grad_input.reshape(volume.shape)
    grad_kernel = jnp.transpose(grad_kernel, (3, 0, 1, 2))[:, None]
    grad_film = smalls_out[1:3, :channels].reshape(2 * channels)
    grad_in_b = smalls_out[3 : 3 + blocks].reshape(hidden)
    return (
        grad_input, grad_kernel, grad_bias[0], grad_film, grad_in_w, grad_in_b, grad_out_w.T
    )


def solution(mesh):
    split = P("groups", "depth", "rows", "cols")
    in_specs = (split, split, P("groups")) + (P(),) * 7
    out_specs = (
        split,
        P("groups", None, None, None, None),
        P("groups"),
        P("groups"),
        P("groups", None),
        P("groups"),
        P("groups", None),
    )
    counts = tuple(mesh.shape[name] for name in ("depth", "rows", "cols"))
    return jax.shard_map(
        functools.partial(local, counts),
        mesh=mesh,
        in_specs=in_specs,
        out_specs=out_specs,
        check_vma=False,
    )
```
